32 devices in a mesh: clu: 4 (over z), row: 8 (over y, x, core).
Axes of the slice: x: 2, y: 2, z: 4, core: 2. Of those that a mesh axis runs over, the one named last changes fastest.
Arguments:
- rhs: float32 [256, 131072], P(None, ('clu', 'row')), may hold values from -6 to 6
- linv: float32 [512, 256, 256], P(('clu', 'row'))
- w_one: float32 [131072, 128], P(('clu', 'row')), may hold values from -1.5 to 1.5
- w_two: float32 [131072, 128], P(('clu', 'row')), may hold values from -1.5 to 1.5
- held: int32 [8], replicated, may hold values from 0 to 7, each once
- ranks: int32 [6], replicated, may hold values from 16 to 128, as said below
Outputs:
- solved: float32 [256, 131072], P(None, ('clu', 'row'))
The draws below stay inside these ranges and needn't reach their ends.
Inputs may be any that keep to these rules, and one draw needn't show every extreme that they name: `ranks`: entries 0 to 3 are the level-one blocks of subtrees in order (two a subtree), the rest the level-two blocks; some entry equals 128. `held`: a permutation of the clusters.
All inputs are finite; a program needn't handle non-finite values.
Results may differ from the reference program's by a relative error of at most 0.0001.
Values sent between devices are 32-bit elements; how exact they have to be, the bound alone decides.
A program may use at most 128 MiB of HBM per device.

```python
import math
import jax
import jax.numpy as jnp
from jax import lax

RANK = 128
LEAF = 256
CLUSTERS = 8
CLUSTER_ROWS = 16384
ORDER = 131072
COLS = 256


def draw_linv(key, part):
    key_diag, key_low = jax.random.split(jax.random.fold_in(key, 11))
    blocks = ORDER // LEAF
    diagonal = jax.random.uniform(key_diag, (blocks, LEAF), jnp.float32, 0.8, 1.6)
    lower = jax.random.normal(key_low, (blocks, LEAF, LEAF), jnp.float32) * (0.6 / LEAF ** 0.5)
    row_ids = jnp.arange(LEAF)[:, None]
    col_ids = jnp.arange(LEAF)[None, :]
    strict = (row_ids > col_ids).astype(jnp.float32)
    ident = (row_ids == col_ids).astype(jnp.float32)
    return lower * strict[None] + diagonal[:, :, None] * ident[None]


def draw_ranks(key, part):
    key_vals, key_spot = jax.random.split(jax.random.fold_in(key, 23))
    count = CLUSTERS * 3 // 4
    values = jax.random.randint(key_vals, (count,), max(1, RANK // 8), RANK + 1, jnp.int32)
    spot = jax.random.randint(key_spot, (), 0, count, jnp.int32)
    return jnp.where(jnp.arange(count) == spot, RANK, values).astype(jnp.int32)


def shard_levels(rng, shape, shards, low, largest):
    level = 1.0
    for dim, shards_of in shards:
        steps = jax.random.uniform(jax.random.fold_in(jax.random.fold_in(rng, 6), dim), (shards_of,), jnp.float32, low / len(shards), largest / len(shards))
        level = level * jnp.repeat(jnp.exp(steps), shape[dim] // shards_of).reshape((-1,) + (1,) * (len(shape) - 1 - dim))
    return level


def gaussian(rng, extent, width, limit, shards=(), kind=jnp.bfloat16):
    values = jax.random.normal(rng, extent, jnp.float32) * width
    if len(shards) > 0:
        values = shard_levels(rng, extent, shards, -0.22, 0.18) * values
    return jnp.clip(values, min=-limit, max=limit).astype(kind)


def setup_inputs(seed: int = 0) -> dict:
    keys = jax.random.split(jax.random.key(seed), 7)
    return {
        "rhs": gaussian(keys[0], (COLS, ORDER), 1.0, 6.0, ((1, 32),), jnp.float32),
        "linv": draw_linv(jax.random.fold_in(keys[6], 71), 0),
        "w_one": gaussian(keys[2], (ORDER, RANK), 0.25, 1.5, ((0, 32),), jnp.float32),
        "w_two": gaussian(keys[3], (ORDER, RANK), 0.25, 1.5, ((0, 32),), jnp.float32),
        "held": jax.random.permutation(keys[4], CLUSTERS).astype(jnp.int32),
        "ranks": draw_ranks(jax.random.fold_in(keys[6], 71), 0),
    }


def leaf_apply(values, inverse):
    blocks = inverse.shape[0]
    leaf_width = inverse.shape[1]
    pieces = values.reshape(values.shape[0], blocks, leaf_width).transpose(1, 0, 2)
    result = jnp.einsum('bcj,bij->bci', pieces, inverse, precision=lax.Precision.HIGHEST)
    return result.transpose(1, 0, 2).reshape(values.shape[0], blocks * leaf_width)

def rank_mask(ranks, block_index):
    return (jnp.arange(RANK) < ranks[block_index]).astype(jnp.float32)

def reference(rhs, linv, w_one, w_two, held, ranks):
    cluster_rows = CLUSTER_ROWS
    scaling = 1.0 / math.sqrt(cluster_rows)
    source = rhs.reshape(COLS, CLUSTERS, cluster_rows).transpose(1, 0, 2)
    inverse = linv.reshape(CLUSTERS, cluster_rows // LEAF, LEAF, LEAF)
    first_weights = w_one.reshape(CLUSTERS, cluster_rows, RANK)
    second_weights = w_two.reshape(CLUSTERS, cluster_rows, RANK)
    solved = jax.vmap(leaf_apply)(source, inverse)
    slot_ids = jnp.arange(CLUSTERS, dtype=jnp.int32)
    where_is = lax.optimization_barrier(jnp.sum(jnp.where(held[None, :] == slot_ids[:, None], slot_ids[None, :], 0), axis=1)).astype(jnp.int32)
    highest = lax.Precision.HIGHEST
    for subtree in range(CLUSTERS // 4):
        group_zero = where_is[4 * subtree]
        group_one = where_is[4 * subtree + 1]
        group_two = where_is[4 * subtree + 2]
        group_three = where_is[4 * subtree + 3]
        coef_one = jnp.dot(solved[group_zero], first_weights[group_zero], precision=highest) * scaling
        coef_one = coef_one * rank_mask(ranks, 2 * subtree)[None, :]
        current = source[group_one] - jnp.dot(coef_one, first_weights[group_one].T, precision=highest)
        solved = solved.at[group_one].set(leaf_apply(current, inverse[group_one]))
        coef_two = jnp.dot(solved[group_zero], second_weights[group_zero], precision=highest) * scaling
        coef_two = coef_two + jnp.dot(solved[group_one], second_weights[group_one], precision=highest) * scaling
        coef_two = coef_two * rank_mask(ranks, CLUSTERS // 2 + subtree)[None, :]
        current = source[group_two] - jnp.dot(coef_two, second_weights[group_two].T, precision=highest)
        solved = solved.at[group_two].set(leaf_apply(current, inverse[group_two]))
        later = source[group_three] - jnp.dot(coef_two, second_weights[group_three].T, precision=highest)
        coef_three = jnp.dot(solved[group_two], first_weights[group_two], precision=highest) * scaling
        coef_three = coef_three * rank_mask(ranks, 2 * subtree + 1)[None, :]
        later = later - jnp.dot(coef_three, first_weights[group_three].T, precision=highest)
        solved = solved.at[group_three].set(leaf_apply(later, inverse[group_three]))
    return solved.transpose(1, 0, 2).reshape(COLS, ORDER)
```

```python
import math

import jax
import jax.numpy as jnp
from jax import lax
from jax.sharding import PartitionSpec as P

HIGH = lax.Precision.HIGH


def shards(rhs, linv, w_one, w_two, held, ranks):
    cols, local_rows = rhs.shape
    blocks, leaf, _ = linv.shape
    rank_width = w_one.shape[1]
    half_rows = lax.axis_size("row") // 2
    slot_count = 2 * lax.axis_size("clu")
    tree_count = slot_count // 4
    scaling = 1.0 / math.sqrt(local_rows * half_rows)
    own_slot = 2 * lax.axis_index("clu") + lax.axis_index("row") // half_rows
    own_cluster = jnp.sum(jnp.where(jnp.arange(slot_count) == own_slot, held, 0))
    position = own_cluster % 4
    subtree = own_cluster // 4
    tree_weights = (jnp.arange(tree_count) == subtree).astype(jnp.float32)

    def mask_for(block_index):
        rank_value = jnp.sum(jnp.where(jnp.arange(ranks.shape[0]) == block_index, ranks, 0))
        return (jnp.arange(rank_width) < rank_value).astype(jnp.float32)[None, :]

    flag = [(position == p).astype(jnp.float32) for p in range(4)]

    weights = jnp.concatenate([w_one, w_two], axis=1)
    leaf_weights = weights.reshape(blocks, leaf, 2 * rank_width)
    pieces = rhs.reshape(cols, blocks, leaf)
    base = jnp.einsum("cbj,bij->cbi", pieces, linv, precision=HIGH)
    spread = jnp.einsum("bij,bjk->bik", linv, leaf_weights, precision=HIGH)
    sums = jnp.dot(base.reshape(cols, local_rows), weights, precision=HIGH) * scaling
    spread = spread.reshape(local_rows, 2 * rank_width)
    second = position == 1
    left = jnp.where(second, spread[:, :rank_width], spread[:, rank_width:])
    right = jnp.where(second, w_two, w_one)
    cross = jnp.einsum("rk,rm->km", left, right, precision=HIGH) * scaling

    one, two = sums[:, :rank_width], sums[:, rank_width:]
    message = jnp.concatenate(
        [flag[0] * one, (flag[0] + flag[1]) * two, flag[2] * one, flag[1] * cross, flag[2] * cross],
        axis=0,
    )
    total = lax.psum(tree_weights[:, None, None] * message[None], ("clu", "row"))
    mine = jnp.sum(tree_weights[:, None, None] * total, axis=0)
    sum_one, sum_two, sum_three = (mine[i * cols : (i + 1) * cols] for i in range(3))
    cross_two, cross_three = (
        mine[3 * cols + i * rank_width : 3 * cols + (i + 1) * rank_width] for i in range(2)
    )
    coef_one = sum_one * mask_for(2 * subtree)
    coef_two = sum_two - jnp.dot(coef_one, cross_two, precision=HIGH)
    coef_two = coef_two * mask_for(slot_count // 2 + subtree)
    coef_three = sum_three - jnp.dot(coef_two, cross_three, precision=HIGH)
    coef_three = coef_three * mask_for(2 * subtree + 1)
    coefs = jnp.concatenate(
        [flag[1] * coef_one + flag[3] * coef_three, (flag[2] + flag[3]) * coef_two], axis=1
    )
    fixes = jnp.einsum("ck,rk->cr", coefs, spread, precision=HIGH)
    return base.reshape(cols, local_rows) - fixes


def solution(mesh):
    in_specs = (
        P(None, ("clu", "row")),
        P(("clu", "row"), None, None),
        P(("clu", "row"), None),
        P(("clu", "row"), None),
        P(),
        P(),
    )
    out_specs = P(None, ("clu", "row"))
    return jax.shard_map(shards, mesh=mesh, in_specs=in_specs, out_specs=out_specs, check_vma=False)
```

```python
import functools
import math

import jax
import jax.numpy as jnp
from jax import lax
from jax.experimental import pallas as pl
from jax.experimental.pallas import tpu as pltpu
from jax.sharding import PartitionSpec as P

MESH = pl.DeviceIdType.MESH
NN = (((1,), (0,)), ((), ()))
NT = (((1,), (1,)), ((), ()))
TN = (((0,), (0,)), ((), ()))


def split(x):
    high = x.astype(jnp.bfloat16)
    return high, (x - high.astype(jnp.float32)).astype(jnp.bfloat16)


def dot3(a, b, dims):
    def one(x, y):
        return lax.dot_general(x, y, dims, preferred_element_type=jnp.float32)

    return one(a[0], b[0]) + (one(a[0], b[1]) + one(a[1], b[0]))


def kernel(
    groups, members, chunks, step,
    held, ranks, rhs, linv, w_one, w_two, out,
    x_buf, l_buf, w_buf, l_hi, l_lo, w_hi, w_lo, s_hi, s_lo,
    g_acc, g_recv, g_sum, g_all, m_acc, m_recv, m_all, m_full, k_send, k_full, k_hi, k_lo,
    in_sems, out_sems, m1_s, m1_r, m2_s, m2_r, m3_s, m3_r, g1_s, g1_r, g2_s, g2_r, k1_s, k1_r, k2_s, k2_r,
):
    cols, rows = x_buf.shape
    blocks, leaf, _ = l_buf.shape
    rank = w_one.shape[1]
    trees = groups // 4
    passes = blocks // step
    width = step * leaf
    scaling = 1.0 / math.sqrt(rows * members)
    clu, row = lax.axis_index("clu"), lax.axis_index("row")
    group = 2 * clu + row // members
    member = row % members
    base = chunks * (group // chunks)
    chunk = group % chunks

    def device_of(g, q):
        return (g // 2, (g % 2) * members + q)

    def loads(c):
        span = pl.ds(pl.multiple_of(c * width, width), width)
        some = pl.ds(c * step, step)
        return (
            pltpu.make_async_copy(linv.at[some], l_buf.at[some], in_sems.at[0, c]),
            pltpu.make_async_copy(w_one.at[span], w_buf.at[span, pl.ds(0, rank)], in_sems.at[1, c]),
            pltpu.make_async_copy(w_two.at[span], w_buf.at[span, pl.ds(rank, rank)], in_sems.at[2, c]),
            pltpu.make_async_copy(rhs.at[:, span], x_buf.at[:, span], in_sems.at[3, c]),
        )

    for c in range(passes):
        for copy in loads(c)[:3]:
            copy.start()
    for c in range(passes):
        loads(c)[3].start()

    other_members = [(member + k) % members for k in range(1, members)]
    other_groups = [(group + k) % groups for k in range(1, groups)]
    block_groups = [base + (chunk + k) % chunks for k in range(1, chunks)]

    barrier = pltpu.get_barrier_semaphore()
    for q in other_members:
        pl.semaphore_signal(barrier, inc=1, device_id=device_of(group, q), device_id_type=MESH)
    for g in other_groups:
        pl.semaphore_signal(barrier, inc=1, device_id=device_of(g, member), device_id_type=MESH)

    def remote(src, dst, send, recv, g, q):
        return pltpu.make_async_remote_copy(
            src_ref=src, dst_ref=dst, send_sem=send, recv_sem=recv,
            device_id=device_of(g, q), device_id_type=MESH,
        )

    sends = []

    def send(*args):
        copy = remote(*args)
        copy.start()
        sends.append(copy)

    position = held[group] % 4
    second = jnp.where(position == 1, 1.0, 0.0).astype(jnp.float32)

    m_acc[...] = jnp.zeros_like(m_acc)
    g_acc[...] = jnp.zeros_like(g_acc)

    def spread(c, carry):
        for copy in loads(c)[:3]:
            copy.wait()
        total = jnp.zeros((rank, rank), jnp.float32)
        for i in range(step):
            b = c * step + i
            span = pl.ds(pl.multiple_of(b * leaf, leaf), leaf)
            weights = w_buf[span, :]
            inverse = split(l_buf[b])
            pair = split(weights)
            l_hi[b], l_lo[b] = inverse
            w_hi[b], w_lo[b] = pair
            result = dot3(inverse, pair, NN)
            s_hi[b], s_lo[b] = split(result)
            left = second * result[:, :rank] + (1.0 - second) * result[:, rank:]
            right = second * weights[:, rank:] + (1.0 - second) * weights[:, :rank]
            total = total + dot3(split(left), split(right), TN)
        m_acc[...] += total.reshape(m_acc.shape)
        return carry

    def solve(c, carry):
        loads(c)[3].wait()
        total = jnp.zeros((cols, 2 * rank), jnp.float32)
        for i in range(step):
            b = c * step + i
            span = pl.ds(pl.multiple_of(b * leaf, leaf), leaf)
            result = dot3(split(x_buf[:, span]), (l_hi[b], l_lo[b]), NT)
            x_buf[:, span] = result
            total = total + dot3(split(result), (w_hi[b], w_lo[b]), NN)
        g_acc[...] += total.reshape(g_acc.shape)
        return carry

    lax.fori_loop(0, passes, spread, 0)
    pl.semaphore_wait(barrier, members - 1 + groups - 1)
    for q in other_members:
        send(m_acc.at[q], m_recv.at[member], m1_s.at[q], m1_r.at[member], group, q)

    lax.fori_loop(0, passes // 2, solve, 0)

    total = m_acc[member]
    for q in other_members:
        remote(m_acc.at[q], m_recv.at[q], m1_s.at[q], m1_r.at[q], group, q).wait_recv()
        total = total + m_recv[q]
    m_all[group] = total * scaling
    for g in other_groups:
        send(m_all.at[group], m_all.at[group], m2_s.at[g], m2_r.at[group], g, member)

    lax.fori_loop(passes // 2, passes, solve, 0)

    for q in other_members:
        send(g_acc.at[q], g_recv.at[member], g1_s.at[q], g1_r.at[member], group, q)

    def weight(g, cluster):
        return jnp.where(held[g] == cluster, 1.0, 0.0).astype(jnp.float32)

    for g in other_groups:
        remote(m_all.at[g], m_all.at[g], m2_s.at[g], m2_r.at[g], g, member).wait_recv()
    for t in range(trees):
        for kind in range(2):
            picked = jnp.zeros(m_all.shape[1:], jnp.float32)
            for g in range(groups):
                picked = picked + weight(g, 4 * t + 1 + kind) * m_all[g]
            m_full[member, 2 * t + kind] = picked
    for q in other_members:
        send(m_full.at[member], m_full.at[member], m3_s.at[q], m3_r.at[member], group, q)

    total = g_acc[member]
    for q in other_members:
        remote(g_acc.at[q], g_recv.at[q], g1_s.at[q], g1_r.at[q], group, q).wait_recv()
        total = total + g_recv[q]
    g_sum[...] = (total * scaling).reshape(g_sum.shape)
    g_all[group] = g_sum[chunk]
    for g in other_groups:
        send(g_sum.at[g % chunks], g_all.at[group], g2_s.at[g], g2_r.at[group], g, member)

    lanes = lax.broadcasted_iota(jnp.int32, (1, rank), 1)

    def mask(index):
        return jnp.where(lanes < ranks[index], 1.0, 0.0).astype(jnp.float32)

    for q in other_members:
        remote(m_full.at[q], m_full.at[q], m3_s.at[q], m3_r.at[q], group, q).wait_recv()
    crosses = [
        split(jnp.concatenate([m_full[q, s] for q in range(members)], axis=0)) for s in range(2 * trees)
    ]
    for g in other_groups:
        remote(g_all.at[g], g_all.at[g], g2_s.at[g], g2_r.at[g], g, member).wait_recv()
    coefs = []
    for t in range(trees):
        zero = jnp.zeros((g_all.shape[1], rank), jnp.float32)
        one, two, three = zero, zero, zero
        for g in range(groups):
            first, last = g_all[g, :, :rank], g_all[g, :, rank:]
            one = one + weight(g, 4 * t) * first
            two = two + (weight(g, 4 * t) + weight(g, 4 * t + 1)) * last
            three = three + weight(g, 4 * t + 2) * first
        one = one * mask(2 * t)
        two = (two - dot3(split(one), crosses[2 * t], NN)) * mask(2 * trees + t)
        three = (three - dot3(split(two), crosses[2 * t + 1], NN)) * mask(2 * t + 1)
        coefs.append((one, two, three))
    for g in range(groups):
        first = jnp.zeros((g_all.shape[1], rank), jnp.float32)
        last = first
        for t in range(trees):
            one, two, three = coefs[t]
            first = first + weight(g, 4 * t + 1) * one + weight(g, 4 * t + 3) * three
            last = last + (weight(g, 4 * t + 2) + weight(g, 4 * t + 3)) * two
        k_send[g, :, :rank] = first
        k_send[g, :, rank:] = last
    k_full[member, chunk] = k_send[group]
    for g in block_groups:
        send(k_send.at[g], k_full.at[member, chunk], k1_s.at[g], k1_r.at[chunk], g, member)
    for g in block_groups:
        c = g % chunks
        remote(k_send.at[g], k_full.at[member, c], k1_s.at[g], k1_r.at[c], g, member).wait_recv()
    for q in other_members:
        send(k_full.at[member], k_full.at[member], k2_s.at[q], k2_r.at[member], group, q)
    for q in other_members:
        remote(k_full.at[q], k_full.at[q], k2_s.at[q], k2_r.at[q], group, q).wait_recv()
    k_hi[...], k_lo[...] = split(k_full[...].reshape(cols, 2 * rank))

    def store(c):
        span = pl.ds(pl.multiple_of(c * width, width), width)
        return pltpu.make_async_copy(x_buf.at[:, span], out.at[:, span], out_sems.at[c])

    def update(c, carry):
        coef = (k_hi[...], k_lo[...])
        for i in range(step):
            b = c * step + i
            span = pl.ds(pl.multiple_of(b * leaf, leaf), leaf)
            x_buf[:, span] = x_buf[:, span] - dot3(coef, (s_hi[b], s_lo[b]), NT)
        store(c).start()
        return carry

    lax.fori_loop(0, passes, update, 0)
    for copy in sends:
        copy.wait_send()
    for c in range(passes):
        store(c).wait()


def shards(rhs, linv, w_one, w_two, held, ranks):
    cols, rows = rhs.shape
    blocks, leaf, _ = linv.shape
    rank = w_one.shape[1]
    groups = 2 * lax.axis_size("clu")
    members = lax.axis_size("row") // 2
    trees = groups // 4
    share = cols // members
    chunks = min(groups, share // 8)
    piece = share // chunks
    part = rank // members
    step = 2
    f32, bf16 = jnp.float32, jnp.bfloat16
    leaf_shape = (blocks, leaf, leaf)
    weight_shape = (blocks, leaf, 2 * rank)
    dma = pltpu.SemaphoreType.DMA
    return pl.pallas_call(
        functools.partial(kernel, groups, members, chunks, step),
        out_shape=jax.ShapeDtypeStruct(rhs.shape, f32),
        in_specs=[pl.BlockSpec(memory_space=pltpu.SMEM)] * 2 + [pl.BlockSpec(memory_space=pl.ANY)] * 4,
        out_specs=pl.BlockSpec(memory_space=pl.ANY),
        scratch_shapes=[
            pltpu.VMEM((cols, rows), f32),
            pltpu.VMEM(leaf_shape, f32),
            pltpu.VMEM((rows, 2 * rank), f32),
            pltpu.VMEM(leaf_shape, bf16),
            pltpu.VMEM(leaf_shape, bf16),
            pltpu.VMEM(weight_shape, bf16),
            pltpu.VMEM(weight_shape, bf16),
            pltpu.VMEM(weight_shape, bf16),
            pltpu.VMEM(weight_shape, bf16),
            pltpu.VMEM((members, share, 2 * rank), f32),
            pltpu.VMEM((members, share, 2 * rank), f32),
            pltpu.VMEM((chunks, piece, 2 * rank), f32),
            pltpu.VMEM((groups, piece, 2 * rank), f32),
            pltpu.VMEM((members, part, rank), f32),
            pltpu.VMEM((members, part, rank), f32),
            pltpu.VMEM((groups, part, rank), f32),
            pltpu.VMEM((members, 2 * trees, part, rank), f32),
            pltpu.VMEM((groups, piece, 2 * rank), f32),
            pltpu.VMEM((members, chunks, piece, 2 * rank), f32),
            pltpu.VMEM((cols, 2 * rank), bf16),
            pltpu.VMEM((cols, 2 * rank), bf16),
            dma((4, blocks // step)),
            dma((blocks // step,)),
            dma((members,)), dma((members,)),
            dma((groups,)), dma((groups,)),
            dma((members,)), dma((members,)),
            dma((members,)), dma((members,)),
            dma((groups,)), dma((groups,)),
            dma((groups,)), dma((chunks,)),
            dma((members,)), dma((members,)),
        ],
        compiler_params=pltpu.CompilerParams(
            collective_id=0, has_side_effects=True, vmem_limit_bytes=48 * 1024 * 1024
        ),
    )(held, ranks, rhs, linv, w_one, w_two)


def solution(mesh):
    in_specs = (
        P(None, ("clu", "row")),
        P(("clu", "row"), None, None),
        P(("clu", "row"), None),
        P(("clu", "row"), None),
        P(),
        P(),
    )
    out_specs = P(None, ("clu", "row"))
    return jax.shard_map(shards, mesh=mesh, in_specs=in_specs, out_specs=out_specs, check_vma=False)
```

```python
import functools
import math

import jax
import jax.numpy as jnp
from jax import lax
from jax.experimental import pallas as pl
from jax.experimental.pallas import tpu as pltpu
from jax.sharding import PartitionSpec as P

MESH = pl.DeviceIdType.MESH
NN = (((1,), (0,)), ((), ()))
NT = (((1,), (1,)), ((), ()))
TN = (((0,), (0,)), ((), ()))


def split(x):
    high = x.astype(jnp.bfloat16)
    return high, (x - high.astype(jnp.float32)).astype(jnp.bfloat16)


def dot3(a, b, dims):
    def one(x, y):
        return lax.dot_general(x, y, dims, preferred_element_type=jnp.float32)

    return one(a[0], b[0]) + (one(a[0], b[1]) + one(a[1], b[0]))


def kernel(
    groups, members, chunks, step,
    held, ranks, rhs, linv, w_one, w_two, z_out, hi_out, lo_out, k_hi, k_lo,
    x_buf, l_buf, w_buf, l_hi, l_lo, w_hi, w_lo, s_hi, s_lo,
    g_acc, g_recv, g_sum, g_all, m_acc, m_recv, m_all, m_full, k_send, k_full,
    in_sems, out_sems, m1_s, m1_r, m2_s, m2_r, m3_s, m3_r, g1_s, g1_r, g2_s, g2_r, k1_s, k1_r, k2_s, k2_r,
):
    cols, rows = x_buf.shape
    blocks, leaf, _ = l_buf.shape
    rank = w_one.shape[1]
    trees = groups // 4
    passes = blocks // step
    width = step * leaf
    scaling = 1.0 / math.sqrt(rows * members)
    clu, row = lax.axis_index("clu"), lax.axis_index("row")
    group = 2 * clu + row // members
    member = row % members
    base = chunks * (group // chunks)
    chunk = group % chunks

    def device_of(g, q):
        return (g // 2, (g % 2) * members + q)

    def loads(c):
        span = pl.ds(pl.multiple_of(c * width, width), width)
        some = pl.ds(c * step, step)
        return (
            pltpu.make_async_copy(linv.at[some], l_buf.at[some], in_sems.at[0, c]),
            pltpu.make_async_copy(w_one.at[span], w_buf.at[span, pl.ds(0, rank)], in_sems.at[1, c]),
            pltpu.make_async_copy(w_two.at[span], w_buf.at[span, pl.ds(rank, rank)], in_sems.at[2, c]),
            pltpu.make_async_copy(rhs.at[:, span], x_buf.at[:, span], in_sems.at[3, c]),
        )

    def stores(c):
        span = pl.ds(pl.multiple_of(c * width, width), width)
        some = pl.ds(c * step, step)
        return (
            pltpu.make_async_copy(x_buf.at[:, span], z_out.at[:, span], out_sems.at[0, c]),
            pltpu.make_async_copy(s_hi.at[some], hi_out.at[some], out_sems.at[1, c]),
            pltpu.make_async_copy(s_lo.at[some], lo_out.at[some], out_sems.at[2, c]),
        )

    for c in range(passes):
        for copy in loads(c)[:3]:
            copy.start()
    for c in range(passes):
        loads(c)[3].start()

    other_members = [(member + k) % members for k in range(1, members)]
    other_groups = [(group + k) % groups for k in range(1, groups)]
    block_groups = [base + (chunk + k) % chunks for k in range(1, chunks)]

    barrier = pltpu.get_barrier_semaphore()
    for q in other_members:
        pl.semaphore_signal(barrier, inc=1, device_id=device_of(group, q), device_id_type=MESH)
    for g in other_groups:
        pl.semaphore_signal(barrier, inc=1, device_id=device_of(g, member), device_id_type=MESH)

    def remote(src, dst, send, recv, g, q):
        return pltpu.make_async_remote_copy(
            src_ref=src, dst_ref=dst, send_sem=send, recv_sem=recv,
            device_id=device_of(g, q), device_id_type=MESH,
        )

    sends = []

    def send(*args):
        copy = remote(*args)
        copy.start()
        sends.append(copy)

    position = held[group] % 4
    second = jnp.where(position == 1, 1.0, 0.0).astype(jnp.float32)

    m_acc[...] = jnp.zeros_like(m_acc)
    g_acc[...] = jnp.zeros_like(g_acc)

    def spread(c, carry):
        for copy in loads(c)[:3]:
            copy.wait()
        total = jnp.zeros((rank, rank), jnp.float32)
        for i in range(step):
            b = c * step + i
            span = pl.ds(pl.multiple_of(b * leaf, leaf), leaf)
            weights = w_buf[span, :]
            inverse = split(l_buf[b])
            pair = split(weights)
            l_hi[b], l_lo[b] = inverse
            w_hi[b], w_lo[b] = pair
            result = dot3(inverse, pair, NN)
            s_hi[b], s_lo[b] = split(result)
            left = second * result[:, :rank] + (1.0 - second) * result[:, rank:]
            right = second * weights[:, rank:] + (1.0 - second) * weights[:, :rank]
            total = total + dot3(split(left), split(right), TN)
        m_acc[...] += total.reshape(m_acc.shape)
        for copy in stores(c)[1:]:
            copy.start()
        return carry

    def solve(c, carry):
        loads(c)[3].wait()
        total = jnp.zeros((cols, 2 * rank), jnp.float32)
        for i in range(step):
            b = c * step + i
            span = pl.ds(pl.multiple_of(b * leaf, leaf), leaf)
            result = dot3(split(x_buf[:, span]), (l_hi[b], l_lo[b]), NT)
            x_buf[:, span] = result
            total = total + dot3(split(result), (w_hi[b], w_lo[b]), NN)
        g_acc[...] += total.reshape(g_acc.shape)
        stores(c)[0].start()
        return carry

    lax.fori_loop(0, passes, spread, 0)
    pl.semaphore_wait(barrier, members - 1 + groups - 1)
    for q in other_members:
        send(m_acc.at[q], m_recv.at[member], m1_s.at[q], m1_r.at[member], group, q)

    lax.fori_loop(0, passes // 2, solve, 0)

    total = m_acc[member]
    for q in other_members:
        remote(m_acc.at[q], m_recv.at[q], m1_s.at[q], m1_r.at[q], group, q).wait_recv()
        total = total + m_recv[q]
    m_all[group] = total * scaling
    for g in other_groups:
        send(m_all.at[group], m_all.at[group], m2_s.at[g], m2_r.at[group], g, member)

    lax.fori_loop(passes // 2, passes, solve, 0)

    for q in other_members:
        send(g_acc.at[q], g_recv.at[member], g1_s.at[q], g1_r.at[member], group, q)

    def weight(g, cluster):
        return jnp.where(held[g] == cluster, 1.0, 0.0).astype(jnp.float32)

    for g in other_groups:
        remote(m_all.at[g], m_all.at[g], m2_s.at[g], m2_r.at[g], g, member).wait_recv()
    for t in range(trees):
        for kind in range(2):
            picked = jnp.zeros(m_all.shape[1:], jnp.float32)
            for g in range(groups):
                picked = picked + weight(g, 4 * t + 1 + kind) * m_all[g]
            m_full[member, 2 * t + kind] = picked
    for q in other_members:
        send(m_full.at[member], m_full.at[member], m3_s.at[q], m3_r.at[member], group, q)

    total = g_acc[member]
    for q in other_members:
        remote(g_acc.at[q], g_recv.at[q], g1_s.at[q], g1_r.at[q], group, q).wait_recv()
        total = total + g_recv[q]
    g_sum[...] = (total * scaling).reshape(g_sum.shape)
    g_all[group] = g_sum[chunk]
    for g in other_groups:
        send(g_sum.at[g % chunks], g_all.at[group], g2_s.at[g], g2_r.at[group], g, member)

    lanes = lax.broadcasted_iota(jnp.int32, (1, rank), 1)

    def mask(index):
        return jnp.where(lanes < ranks[index], 1.0, 0.0).astype(jnp.float32)

    for q in other_members:
        remote(m_full.at[q], m_full.at[q], m3_s.at[q], m3_r.at[q], group, q).wait_recv()
    crosses = [
        split(jnp.concatenate([m_full[q, s] for q in range(members)], axis=0)) for s in range(2 * trees)
    ]
    for g in other_groups:
        remote(g_all.at[g], g_all.at[g], g2_s.at[g], g2_r.at[g], g, member).wait_recv()
    coefs = []
    for t in range(trees):
        zero = jnp.zeros((g_all.shape[1], rank), jnp.float32)
        one, two, three = zero, zero, zero
        for g in range(groups):
            first, last = g_all[g, :, :rank], g_all[g, :, rank:]
            one = one + weight(g, 4 * t) * first
            two = two + (weight(g, 4 * t) + weight(g, 4 * t + 1)) * last
            three = three + weight(g, 4 * t + 2) * first
        one = one * mask(2 * t)
        two = (two - dot3(split(one), crosses[2 * t], NN)) * mask(2 * trees + t)
        three = (three - dot3(split(two), crosses[2 * t + 1], NN)) * mask(2 * t + 1)
        coefs.append((one, two, three))
    for g in range(groups):
        first = jnp.zeros((g_all.shape[1], rank), jnp.float32)
        last = first
        for t in range(trees):
            one, two, three = coefs[t]
            first = first + weight(g, 4 * t + 1) * one + weight(g, 4 * t + 3) * three
            last = last + (weight(g, 4 * t + 2) + weight(g, 4 * t + 3)) * two
        k_send[g, :, :rank] = first
        k_send[g, :, rank:] = last
    k_full[member, chunk] = k_send[group]
    for g in block_groups:
        send(k_send.at[g], k_full.at[member, chunk], k1_s.at[g], k1_r.at[chunk], g, member)
    for g in block_groups:
        c = g % chunks
        remote(k_send.at[g], k_full.at[member, c], k1_s.at[g], k1_r.at[c], g, member).wait_recv()
    for q in other_members:
        send(k_full.at[member], k_full.at[member], k2_s.at[q], k2_r.at[member], group, q)
    for q in other_members:
        remote(k_full.at[q], k_full.at[q], k2_s.at[q], k2_r.at[q], group, q).wait_recv()
    k_hi[...], k_lo[...] = split(k_full[...].reshape(cols, 2 * rank))

    for copy in sends:
        copy.wait_send()
    for c in range(passes):
        for copy in stores(c):
            copy.wait()


def update(base, high, low, coef_high, coef_low, out):
    leaf = high.shape[1]
    coef = (coef_high[...], coef_low[...])
    for i in range(high.shape[0]):
        span = pl.ds(i * leaf, leaf)
        out[:, span] = base[:, span] - dot3(coef, (high[i], low[i]), NT)


def shards(rhs, linv, w_one, w_two, held, ranks):
    cols, rows = rhs.shape
    blocks, leaf, _ = linv.shape
    rank = w_one.shape[1]
    groups = 2 * lax.axis_size("clu")
    members = lax.axis_size("row") // 2
    trees = groups // 4
    share = cols // members
    chunks = min(groups, share // 8)
    piece = share // chunks
    part = rank // members
    step = 2
    f32, bf16 = jnp.float32, jnp.bfloat16
    leaf_shape = (blocks, leaf, leaf)
    weight_shape = (blocks, leaf, 2 * rank)
    dma = pltpu.SemaphoreType.DMA
    hbm = pl.BlockSpec(memory_space=pl.ANY)
    base, high, low, coef_high, coef_low = pl.pallas_call(
        functools.partial(kernel, groups, members, chunks, step),
        out_shape=[
            jax.ShapeDtypeStruct(rhs.shape, f32),
            jax.ShapeDtypeStruct(weight_shape, bf16),
            jax.ShapeDtypeStruct(weight_shape, bf16),
            jax.ShapeDtypeStruct((cols, 2 * rank), bf16),
            jax.ShapeDtypeStruct((cols, 2 * rank), bf16),
        ],
        in_specs=[pl.BlockSpec(memory_space=pltpu.SMEM)] * 2 + [pl.BlockSpec(memory_space=pl.ANY)] * 4,
        out_specs=[hbm] * 3 + [pl.BlockSpec(memory_space=pltpu.VMEM)] * 2,
        scratch_shapes=[
            pltpu.VMEM((cols, rows), f32),
            pltpu.VMEM(leaf_shape, f32),
            pltpu.VMEM((rows, 2 * rank), f32),
            pltpu.VMEM(leaf_shape, bf16),
            pltpu.VMEM(leaf_shape, bf16),
            pltpu.VMEM(weight_shape, bf16),
            pltpu.VMEM(weight_shape, bf16),
            pltpu.VMEM(weight_shape, bf16),
            pltpu.VMEM(weight_shape, bf16),
            pltpu.VMEM((members, share, 2 * rank), f32),
            pltpu.VMEM((members, share, 2 * rank), f32),
            pltpu.VMEM((chunks, piece, 2 * rank), f32),
            pltpu.VMEM((groups, piece, 2 * rank), f32),
            pltpu.VMEM((members, part, rank), f32),
            pltpu.VMEM((members, part, rank), f32),
            pltpu.VMEM((groups, part, rank), f32),
            pltpu.VMEM((members, 2 * trees, part, rank), f32),
            pltpu.VMEM((groups, piece, 2 * rank), f32),
            pltpu.VMEM((members, chunks, piece, 2 * rank), f32),
            dma((4, blocks // step)),
            dma((3, blocks // step)),
            dma((members,)), dma((members,)),
            dma((groups,)), dma((groups,)),
            dma((members,)), dma((members,)),
            dma((members,)), dma((members,)),
            dma((groups,)), dma((groups,)),
            dma((groups,)), dma((chunks,)),
            dma((members,)), dma((members,)),
        ],
        compiler_params=pltpu.CompilerParams(
            collective_id=0, has_side_effects=True, vmem_limit_bytes=60 * 1024 * 1024
        ),
    )(held, ranks, rhs, linv, w_one, w_two)
    wide = pl.BlockSpec((cols, step * leaf), lambda c: (0, c))
    stack = pl.BlockSpec((step, leaf, 2 * rank), lambda c: (c, 0, 0))
    whole = pl.BlockSpec((cols, 2 * rank), lambda c: (0, 0))
    return pl.pallas_call(
        update,
        grid=(blocks // step,),
        out_shape=jax.ShapeDtypeStruct(rhs.shape, f32),
        in_specs=[wide, stack, stack, whole, whole],
        out_specs=wide,
    )(base, high, low, coef_high, coef_low)


def solution(mesh):
    in_specs = (
        P(None, ("clu", "row")),
        P(("clu", "row"), None, None),
        P(("clu", "row"), None),
        P(("clu", "row"), None),
        P(),
        P(),
    )
    out_specs = P(None, ("clu", "row"))
    return jax.shard_map(shards, mesh=mesh, in_specs=in_specs, out_specs=out_specs, check_vma=False)
```

```python
import functools
import math

import jax
import jax.numpy as jnp
from jax import lax
from jax.experimental import pallas as pl
from jax.experimental.pallas import tpu as pltpu
from jax.sharding import PartitionSpec as P

MESH = pl.DeviceIdType.MESH
NN = (((1,), (0,)), ((), ()))
NT = (((1,), (1,)), ((), ()))
TN = (((0,), (0,)), ((), ()))


def split(x):
    high = x.astype(jnp.bfloat16)
    return high, (x - high.astype(jnp.float32)).astype(jnp.bfloat16)


def dot3(a, b, dims):
    def one(x, y):
        return lax.dot_general(x, y, dims, preferred_element_type=jnp.float32)

    return one(a[0], b[0]) + (one(a[0], b[1]) + one(a[1], b[0]))


def kernel(
    groups, members, chunks, step,
    held, ranks, rhs, linv, w_one, w_two, z_out, hi_out, lo_out, k_hi, k_lo,
    x_buf, l_buf, w_buf, l_hi, l_lo, w_hi, w_lo, s_hi, s_lo,
    g_acc, g_recv, g_sum, g_all, m_acc, m_recv, m_all, m_full, k_send, k_full,
    in_sems, out_sems, m1_s, m1_r, m2_s, m2_r, m3_s, m3_r, g1_s, g1_r, g2_s, g2_r, k1_s, k1_r, k2_s, k2_r,
):
    cols, rows = x_buf.shape
    blocks, leaf, _ = l_buf.shape
    rank = w_one.shape[1]
    trees = groups // 4
    passes = blocks // step
    width = step * leaf
    scaling = 1.0 / math.sqrt(rows * members)
    clu, row = lax.axis_index("clu"), lax.axis_index("row")
    group = 2 * clu + row // members
    member = row % members
    base = chunks * (group // chunks)
    chunk = group % chunks

    def device_of(g, q):
        return (g // 2, (g % 2) * members + q)

    def loads(c):
        span = pl.ds(pl.multiple_of(c * width, width), width)
        some = pl.ds(c * step, step)
        return (
            pltpu.make_async_copy(linv.at[some], l_buf.at[some], in_sems.at[0, c]),
            pltpu.make_async_copy(w_one.at[span], w_buf.at[span, pl.ds(0, rank)], in_sems.at[1, c]),
            pltpu.make_async_copy(w_two.at[span], w_buf.at[span, pl.ds(rank, rank)], in_sems.at[2, c]),
            pltpu.make_async_copy(rhs.at[:, span], x_buf.at[:, span], in_sems.at[3, c]),
        )

    def stores(c):
        span = pl.ds(pl.multiple_of(c * width, width), width)
        some = pl.ds(c * step, step)
        return (
            pltpu.make_async_copy(x_buf.at[:, span], z_out.at[:, span], out_sems.at[0, c]),
            pltpu.make_async_copy(s_hi.at[some], hi_out.at[some], out_sems.at[1, c]),
            pltpu.make_async_copy(s_lo.at[some], lo_out.at[some], out_sems.at[2, c]),
        )

    for c in range(passes):
        for copy in loads(c)[:3]:
            copy.start()
    for c in range(passes):
        loads(c)[3].start()

    other_members = [(member + k) % members for k in range(1, members)]
    other_groups = [(group + k) % groups for k in range(1, groups)]
    block_groups = [base + (chunk + k) % chunks for k in range(1, chunks)]

    barrier = pltpu.get_barrier_semaphore()
    for q in other_members:
        pl.semaphore_signal(barrier, inc=1, device_id=device_of(group, q), device_id_type=MESH)
    for g in other_groups:
        pl.semaphore_signal(barrier, inc=1, device_id=device_of(g, member), device_id_type=MESH)

    def remote(src, dst, send, recv, g, q):
        return pltpu.make_async_remote_copy(
            src_ref=src, dst_ref=dst, send_sem=send, recv_sem=recv,
            device_id=device_of(g, q), device_id_type=MESH,
        )

    sends = []

    def send(*args):
        copy = remote(*args)
        copy.start()
        sends.append(copy)

    position = held[group] % 4
    second = jnp.where(position == 1, 1.0, 0.0).astype(jnp.float32)

    m_acc[...] = jnp.zeros_like(m_acc)
    g_acc[...] = jnp.zeros_like(g_acc)

    def spread(c, carry):
        for copy in loads(c)[:3]:
            copy.wait()
        total = jnp.zeros((rank, rank), jnp.float32)
        for i in range(step):
            b = c * step + i
            span = pl.ds(pl.multiple_of(b * leaf, leaf), leaf)
            weights = w_buf[span, :]
            inverse = split(l_buf[b])
            pair = split(weights)
            l_hi[b], l_lo[b] = inverse
            w_hi[b], w_lo[b] = pair
            result = dot3(inverse, pair, NN)
            s_hi[b], s_lo[b] = split(result)
            left = second * result[:, :rank] + (1.0 - second) * result[:, rank:]
            right = second * weights[:, rank:] + (1.0 - second) * weights[:, :rank]
            total = total + dot3(split(left), split(right), TN)
        m_acc[...] += total.reshape(m_acc.shape)
        for copy in stores(c)[1:]:
            copy.start()
        return carry

    def solve(c, carry):
        loads(c)[3].wait()
        total = jnp.zeros((cols, 2 * rank), jnp.float32)
        for i in range(step):
            b = c * step + i
            span = pl.ds(pl.multiple_of(b * leaf, leaf), leaf)
            result = dot3(split(x_buf[:, span]), (l_hi[b], l_lo[b]), NT)
            x_buf[:, span] = result
            total = total + dot3(split(result), (w_hi[b], w_lo[b]), NN)
        g_acc[...] += total.reshape(g_acc.shape)
        stores(c)[0].start()
        return carry

    lax.fori_loop(0, passes, spread, 0)
    pl.semaphore_wait(barrier, members - 1 + groups - 1)
    for q in other_members:
        send(m_acc.at[q], m_recv.at[member], m1_s.at[q], m1_r.at[member], group, q)

    lax.fori_loop(0, passes // 2, solve, 0)

    total = m_acc[member]
    for q in other_members:
        remote(m_acc.at[q], m_recv.at[q], m1_s.at[q], m1_r.at[q], group, q).wait_recv()
        total = total + m_recv[q]
    m_all[group] = total * scaling
    for g in other_groups:
        send(m_all.at[group], m_all.at[group], m2_s.at[g], m2_r.at[group], g, member)

    lax.fori_loop(passes // 2, passes, solve, 0)

    for q in other_members:
        send(g_acc.at[q], g_recv.at[member], g1_s.at[q], g1_r.at[member], group, q)

    def weight(g, cluster):
        return jnp.where(held[g] == cluster, 1.0, 0.0).astype(jnp.float32)

    for g in other_groups:
        remote(m_all.at[g], m_all.at[g], m2_s.at[g], m2_r.at[g], g, member).wait_recv()
    for t in range(trees):
        for kind in range(2):
            picked = jnp.zeros(m_all.shape[1:], jnp.float32)
            for g in range(groups):
                picked = picked + weight(g, 4 * t + 1 + kind) * m_all[g]
            m_full[member, 2 * t + kind] = picked
    for q in other_members:
        send(m_full.at[member], m_full.at[member], m3_s.at[q], m3_r.at[member], group, q)

    total = g_acc[member]
    for q in other_members:
        remote(g_acc.at[q], g_recv.at[q], g1_s.at[q], g1_r.at[q], group, q).wait_recv()
        total = total + g_recv[q]
    g_sum[...] = (total * scaling).reshape(g_sum.shape)
    g_all[group] = g_sum[chunk]
    for g in other_groups:
        send(g_sum.at[g % chunks], g_all.at[group], g2_s.at[g], g2_r.at[group], g, member)

    lanes = lax.broadcasted_iota(jnp.int32, (1, rank), 1)

    def mask(index):
        return jnp.where(lanes < ranks[index], 1.0, 0.0).astype(jnp.float32)

    for q in other_members:
        remote(m_full.at[q], m_full.at[q], m3_s.at[q], m3_r.at[q], group, q).wait_recv()
    crosses = [
        split(jnp.concatenate([m_full[q, s] for q in range(members)], axis=0)) for s in range(2 * trees)
    ]
    for g in other_groups:
        remote(g_all.at[g], g_all.at[g], g2_s.at[g], g2_r.at[g], g, member).wait_recv()
    coefs = []
    for t in range(trees):
        zero = jnp.zeros((g_all.shape[1], rank), jnp.float32)
        one, two, three = zero, zero, zero
        for g in range(groups):
            first, last = g_all[g, :, :rank], g_all[g, :, rank:]
            one = one + weight(g, 4 * t) * first
            two = two + (weight(g, 4 * t) + weight(g, 4 * t + 1)) * last
            three = three + weight(g, 4 * t + 2) * first
        one = one * mask(2 * t)
        two = (two - dot3(split(one), crosses[2 * t], NN)) * mask(2 * trees + t)
        three = (three - dot3(split(two), crosses[2 * t + 1], NN)) * mask(2 * t + 1)
        coefs.append((one, two, three))
    for g in range(groups):
        first = jnp.zeros((g_all.shape[1], rank), jnp.float32)
        last = first
        for t in range(trees):
            one, two, three = coefs[t]
            first = first + weight(g, 4 * t + 1) * one + weight(g, 4 * t + 3) * three
            last = last + (weight(g, 4 * t + 2) + weight(g, 4 * t + 3)) * two
        k_send[g, :, :rank] = first
        k_send[g, :, rank:] = last
    k_full[member, chunk] = k_send[group]
    for g in block_groups:
        send(k_send.at[g], k_full.at[member, chunk], k1_s.at[g], k1_r.at[chunk], g, member)
    for g in block_groups:
        c = g % chunks
        remote(k_send.at[g], k_full.at[member, c], k1_s.at[g], k1_r.at[c], g, member).wait_recv()
    for q in other_members:
        send(k_full.at[member], k_full.at[member], k2_s.at[q], k2_r.at[member], group, q)
    for q in other_members:
        remote(k_full.at[q], k_full.at[q], k2_s.at[q], k2_r.at[q], group, q).wait_recv()
    k_hi[...], k_lo[...] = split(k_full[...].reshape(cols, 2 * rank))

    for copy in sends:
        copy.wait_send()
    for c in range(passes):
        for copy in stores(c):
            copy.wait()


def update(step, base, high, low, coef_high, coef_low, out, x_buf, s_hi, s_lo, in_sems, out_sems):
    blocks, leaf, _ = s_hi.shape
    passes = blocks // step
    width = step * leaf

    def loads(c):
        span = pl.ds(pl.multiple_of(c * width, width), width)
        some = pl.ds(c * step, step)
        return (
            pltpu.make_async_copy(high.at[some], s_hi.at[some], in_sems.at[0, c]),
            pltpu.make_async_copy(low.at[some], s_lo.at[some], in_sems.at[1, c]),
            pltpu.make_async_copy(base.at[:, span], x_buf.at[:, span], in_sems.at[2, c]),
        )

    def store(c):
        span = pl.ds(pl.multiple_of(c * width, width), width)
        return pltpu.make_async_copy(x_buf.at[:, span], out.at[:, span], out_sems.at[c])

    for c in range(passes):
        for copy in loads(c):
            copy.start()
    coef = jnp.concatenate([coef_high[...], coef_high[...], coef_low[...]], axis=1)

    def work(c, carry):
        for copy in loads(c):
            copy.wait()
        for i in range(step):
            b = c * step + i
            span = pl.ds(pl.multiple_of(b * leaf, leaf), leaf)
            bases = jnp.concatenate([s_hi[b], s_lo[b], s_hi[b]], axis=1)
            fix = lax.dot_general(coef, bases, NT, preferred_element_type=jnp.float32)
            x_buf[:, span] = x_buf[:, span] - fix
        store(c).start()
        return carry

    lax.fori_loop(0, passes, work, 0)
    for c in range(passes):
        store(c).wait()


def shards(rhs, linv, w_one, w_two, held, ranks):
    cols, rows = rhs.shape
    blocks, leaf, _ = linv.shape
    rank = w_one.shape[1]
    groups = 2 * lax.axis_size("clu")
    members = lax.axis_size("row") // 2
    trees = groups // 4
    share = cols // members
    chunks = min(groups, share // 8)
    piece = share // chunks
    part = rank // members
    step = 2
    f32, bf16 = jnp.float32, jnp.bfloat16
    leaf_shape = (blocks, leaf, leaf)
    weight_shape = (blocks, leaf, 2 * rank)
    dma = pltpu.SemaphoreType.DMA
    hbm = pl.BlockSpec(memory_space=pl.ANY)
    base, high, low, coef_high, coef_low = pl.pallas_call(
        functools.partial(kernel, groups, members, chunks, step),
        out_shape=[
            jax.ShapeDtypeStruct(rhs.shape, f32),
            jax.ShapeDtypeStruct(weight_shape, bf16),
            jax.ShapeDtypeStruct(weight_shape, bf16),
            jax.ShapeDtypeStruct((cols, 2 * rank), bf16),
            jax.ShapeDtypeStruct((cols, 2 * rank), bf16),
        ],
        in_specs=[pl.BlockSpec(memory_space=pltpu.SMEM)] * 2 + [pl.BlockSpec(memory_space=pl.ANY)] * 4,
        out_specs=[hbm] * 3 + [pl.BlockSpec(memory_space=pltpu.VMEM)] * 2,
        scratch_shapes=[
            pltpu.VMEM((cols, rows), f32),
            pltpu.VMEM(leaf_shape, f32),
            pltpu.VMEM((rows, 2 * rank), f32),
            pltpu.VMEM(leaf_shape, bf16),
            pltpu.VMEM(leaf_shape, bf16),
            pltpu.VMEM(weight_shape, bf16),
            pltpu.VMEM(weight_shape, bf16),
            pltpu.VMEM(weight_shape, bf16),
            pltpu.VMEM(weight_shape, bf16),
            pltpu.VMEM((members, share, 2 * rank), f32),
            pltpu.VMEM((members, share, 2 * rank), f32),
            pltpu.VMEM((chunks, piece, 2 * rank), f32),
            pltpu.VMEM((groups, piece, 2 * rank), f32),
            pltpu.VMEM((members, part, rank), f32),
            pltpu.VMEM((members, part, rank), f32),
            pltpu.VMEM((groups, part, rank), f32),
            pltpu.VMEM((members, 2 * trees, part, rank), f32),
            pltpu.VMEM((groups, piece, 2 * rank), f32),
            pltpu.VMEM((members, chunks, piece, 2 * rank), f32),
            dma((4, blocks // step)),
            dma((3, blocks // step)),
            dma((members,)), dma((members,)),
            dma((groups,)), dma((groups,)),
            dma((members,)), dma((members,)),
            dma((members,)), dma((members,)),
            dma((groups,)), dma((groups,)),
            dma((groups,)), dma((chunks,)),
            dma((members,)), dma((members,)),
        ],
        compiler_params=pltpu.CompilerParams(
            collective_id=0, has_side_effects=True, vmem_limit_bytes=60 * 1024 * 1024
        ),
    )(held, ranks, rhs, linv, w_one, w_two)
    return pl.pallas_call(
        functools.partial(update, step),
        out_shape=jax.ShapeDtypeStruct(rhs.shape, f32),
        in_specs=[hbm] * 3 + [pl.BlockSpec(memory_space=pltpu.VMEM)] * 2,
        out_specs=hbm,
        scratch_shapes=[
            pltpu.VMEM((cols, rows), f32),
            pltpu.VMEM(weight_shape, bf16),
            pltpu.VMEM(weight_shape, bf16),
            dma((3, blocks // step)),
            dma((blocks // step,)),
        ],
        compiler_params=pltpu.CompilerParams(vmem_limit_bytes=60 * 1024 * 1024),
    )(base, high, low, coef_high, coef_low)


def solution(mesh):
    in_specs = (
        P(None, ("clu", "row")),
        P(("clu", "row"), None, None),
        P(("clu", "row"), None),
        P(("clu", "row"), None),
        P(),
        P(),
    )
    out_specs = P(None, ("clu", "row"))
    return jax.shard_map(shards, mesh=mesh, in_specs=in_specs, out_specs=out_specs, check_vma=False)
```
